256 devices in a mesh: branch: 64 (over x, z, core), sub: 4 (over y).
Axes of the slice: x: 4, y: 4, z: 8, core: 2. Of those that a mesh axis runs over, the one named last changes fastest.
Arguments:
- vectors: float32 [9216, 16, 128], P(('branch', 'sub')), may hold values from -6 to 6
- leaf_basis: float32 [9216, 64, 128], P(('branch', 'sub')), may hold values from -0.5 to 0.5
- near_index: int32 [9216, 3], P(('branch', 'sub')), may hold values from 0 to 9215, as said below
- near_blocks: float32 [9216, 3, 128, 128], P(('branch', 'sub')), may hold values from -0.3125 to 0.3125
- coupling_index: int32 [9216, 4], P(('branch', 'sub')), may hold values from 0 to 9215, as said below
- coupling_blocks: float32 [9216, 4, 64, 64], P(('branch', 'sub')), may hold values from -0.375 to 0.375
- leaf_transfer: float32 [9216, 64, 64], P(('branch', 'sub')), may hold values from -0.125 to 0.125
- cluster_transfer: float32 [256, 64, 64], P(('branch', 'sub')), may hold values from -0.375 to 0.375
- branch_index: int32 [64, 16], P('branch'), may hold values from 0 to 63, as said below
- branch_blocks: float32 [64, 16, 64, 64], P('branch'), may hold values from -0.1875 to 0.1875
Outputs:
- product: float32 [9216, 16, 128], P(('branch', 'sub'))
The draws below stay inside these ranges and needn't reach their ends.
Inputs may be any that keep to these rules, and one draw needn't show every extreme that they name: `near_index`: entry 0 of row l is l itself; every entry of row l lies within 36 of l. `coupling_index`: every entry of row l lies within 36 of l. `branch_index`: the entries of a row are distinct and differ from the row's own branch cluster.
All inputs are finite; a program needn't handle non-finite values.
Results may differ from the reference program's by a relative error of at most 0.000067.
Values sent between devices are 32-bit elements; how exact they have to be, the bound alone decides.
A program may use at most 64 MiB of HBM per device.

```python
import jax
import jax.numpy as jnp
from jax import lax

P_SIZE = 128
R = 64
NV = 16
LEAF_DEV = 36
NEAR = 3
COUP = 4
HALO = 36
MEMBERS = 4
BRANCHES = 64
LEAVES = 9216
TOP_COUP = 16


def within_reach(key, columns):
    offsets = jax.random.randint(key, (LEAVES, columns), -HALO, HALO + 1, dtype=jnp.int32)
    rows = jnp.arange(LEAVES, dtype=jnp.int32)[:, None]
    return jnp.clip(rows + offsets, 0, LEAVES - 1).astype(jnp.int32)


def draw_near_index(key, part):
    listed = within_reach(jax.random.fold_in(key, 11), NEAR)
    rows = jnp.arange(LEAVES, dtype=jnp.int32)
    return listed.at[:, 0].set(rows)


def draw_coupling_index(key, part):
    return within_reach(jax.random.fold_in(key, 23), COUP)


def draw_branch_index(key, part):
    keys = jax.random.split(jax.random.fold_in(key, 37), BRANCHES)
    offsets = jax.vmap(lambda one: jax.random.permutation(one, BRANCHES - 1)[:TOP_COUP])(keys) + 1
    rows = jnp.arange(BRANCHES, dtype=jnp.int32)[:, None]
    return ((rows + offsets.astype(jnp.int32)) % BRANCHES).astype(jnp.int32)


def block_scale(rng, shape, shards, smallest, top_value):
    def one(dim, parts):
        steps = jax.random.uniform(jax.random.fold_in(jax.random.fold_in(rng, 6), dim), (parts,), jnp.float32, smallest / len(shards), top_value / len(shards))
        return jnp.repeat(jnp.exp(steps), shape[dim] // parts).reshape((-1,) + (1,) * (len(shape) - dim - 1))

    loudness = one(*shards[0])
    for cut in shards[1:]:
        loudness = loudness * one(*cut)
    return loudness


def bell_draw(key, dims, deviation, reach, cuts=(), held_as=jnp.bfloat16):
    entries = jax.random.normal(key, dims, jnp.float32) * deviation
    if len(cuts) > 0:
        entries = block_scale(key, dims, cuts, -0.22, 0.18) * entries
    return jnp.clip(entries, min=-reach, max=reach).astype(held_as)


def setup_inputs(seed: int = 0) -> dict:
    splits = jax.random.split(jax.random.key(seed), 11)
    vectors = bell_draw(splits[0], (LEAVES, NV, P_SIZE), 1.0, 6.0, ((0, 256),), jnp.float32)
    leaf_basis = bell_draw(splits[1], (LEAVES, R, P_SIZE), P_SIZE ** -0.5, 0.5, ((0, 256),), jnp.float32)
    near_index = draw_near_index(jax.random.fold_in(splits[10], 71), 0)
    near_blocks = bell_draw(splits[3], (LEAVES, NEAR, P_SIZE, P_SIZE), (NEAR * P_SIZE) ** -0.5, 0.3125, ((0, 256),), jnp.float32)
    coupling_index = draw_coupling_index(jax.random.fold_in(splits[10], 71), 0)
    coupling_blocks = bell_draw(splits[5], (LEAVES, COUP, R, R), (COUP * R) ** -0.5, 0.375, ((0, 256),), jnp.float32)
    leaf_transfer = bell_draw(splits[6], (LEAVES, R, R), (R * LEAF_DEV) ** -0.5, 0.125, ((0, 256),), jnp.float32)
    cluster_transfer = bell_draw(splits[7], (LEAVES // LEAF_DEV, R, R), (R * MEMBERS) ** -0.5, 0.375, ((0, 256),), jnp.float32)
    branch_index = draw_branch_index(jax.random.fold_in(splits[10], 71), 0)
    branch_blocks = bell_draw(splits[9], (BRANCHES, TOP_COUP, R, R), (R * TOP_COUP) ** -0.5, 0.1875, ((0, 64),), jnp.float32)
    return dict(vectors=vectors, leaf_basis=leaf_basis, near_index=near_index, near_blocks=near_blocks, coupling_index=coupling_index, coupling_blocks=coupling_blocks, leaf_transfer=leaf_transfer, cluster_transfer=cluster_transfer, branch_index=branch_index, branch_blocks=branch_blocks)


highest = lax.Precision.HIGHEST


def reference(vectors, leaf_basis, near_index, near_blocks, coupling_index, coupling_blocks, leaf_transfer, cluster_transfer, branch_index, branch_blocks):
    clusters = LEAVES // LEAF_DEV
    coeffs = jnp.einsum('lrp,lvp->lvr', leaf_basis, vectors, precision=highest)
    near_rows = vectors[near_index]
    near_part = jnp.einsum('lkpq,lkvq->lvp', near_blocks, near_rows, precision=highest)
    leaf_far = jnp.einsum('lkrs,lkvs->lvr', coupling_blocks, coeffs[coupling_index], precision=highest)
    grouped_transfer = leaf_transfer.reshape(clusters, LEAF_DEV, R, R)
    cluster = jnp.einsum('dcrs,dcvs->dvr', grouped_transfer, coeffs.reshape(clusters, LEAF_DEV, NV, R), precision=highest)
    grouped_cluster = cluster_transfer.reshape(BRANCHES, MEMBERS, R, R)
    node = jnp.einsum('bsrt,bsvt->bvr', grouped_cluster, cluster.reshape(BRANCHES, MEMBERS, NV, R), precision=highest)
    branch_far = jnp.einsum('bkrs,bkvs->bvr', branch_blocks, node[branch_index], precision=highest)
    cluster_down = jnp.einsum('bsrt,bvr->bsvt', grouped_cluster, branch_far, precision=highest).reshape(clusters, NV, R)
    leaf_total = leaf_far + jnp.einsum('dcrs,dvr->dcvs', grouped_transfer, cluster_down, precision=highest).reshape(LEAVES, NV, R)
    return near_part + jnp.einsum('lrp,lvr->lvp', leaf_basis, leaf_total, precision=highest)
```

```python
import jax
import jax.numpy as jnp
from jax import lax
from jax.experimental import pallas as pl
from jax.experimental.pallas import tpu as pltpu
from jax.sharding import PartitionSpec as P

MESH = pl.DeviceIdType.MESH
NT = (((1,), (1,)), ((), ()))
NN = (((1,), (0,)), ((), ()))
XS, ZS, CS, YS = 4, 8, 2, 4
L = 36
GROUP = 6


def split(x):
    hi = x.astype(jnp.bfloat16)
    lo = (x - hi.astype(jnp.float32)).astype(jnp.bfloat16)
    return hi, lo


def mm(a, b, dims):
    return lax.dot_general(a, b, dims, preferred_element_type=jnp.float32)


def dot3(a, b, dims):
    ah, al = split(a)
    bh, bl = split(b)
    rows = a.shape[0]
    both = mm(jnp.concatenate([ah, al], axis=0), bh, dims)
    return both[:rows] + (both[rows:] + mm(ah, bl, dims))


def pack(c):
    return jnp.concatenate([c[:8], c[8:]], axis=1)


def unpack(p):
    return jnp.concatenate([p[:, :64], p[:, 64:]], axis=0)


def groups(body, init=None):
    def step(g, carry):
        return body([g * GROUP + i for i in range(GROUP)], carry)

    return lax.fori_loop(0, L // GROUP, step, init)


def kernel(
    near_index,
    coup_index,
    branch_index,
    vec_hbm,
    basis_hbm,
    near_hbm,
    coup_hbm,
    lt_hbm,
    ct_hbm,
    bb_hbm,
    out,
    wide,
    cw,
    basis,
    near,
    coup,
    lt,
    ct,
    bb,
    shares,
    nodes,
    down,
    local_sem,
    halo_send,
    halo_recv,
    tree_send,
    tree_recv,
):
    b = lax.axis_index("branch")
    y = lax.axis_index("sub")
    core = lax.rem(b, CS)
    z = lax.rem(lax.div(b, CS), ZS)
    x = lax.div(b, CS * ZS)
    flat = b * YS + y
    total = XS * ZS * CS * YS
    right = lax.rem(flat + 1, total)
    left = lax.rem(flat + total - 1, total)
    right = (lax.div(right, YS), lax.rem(right, YS))
    left = (lax.div(left, YS), lax.rem(left, YS))
    y_peers = [(b, lax.rem(y + j, YS)) for j in range(1, YS)]
    z_peers = [((x * ZS + lax.rem(z + j, ZS)) * CS + core, y) for j in range(1, ZS)]
    x_peers = [((lax.rem(x + j, XS) * ZS + z) * CS + core, y) for j in range(1, XS)]
    core_peers = [(b + 1 - 2 * core, y)]

    def local(src, dst, n):
        return pltpu.make_async_copy(src, dst, local_sem.at[n])

    loads = [
        local(vec_hbm, wide.at[pl.ds(L, L)], 0),
        local(basis_hbm, basis, 1),
        local(lt_hbm, lt, 2),
        local(ct_hbm, ct, 3),
        local(bb_hbm, bb, 4),
        local(near_hbm, near, 5),
        local(coup_hbm, coup, 6),
    ]
    for load in loads:
        load.start()

    barrier = pltpu.get_barrier_semaphore()
    peers = [right, left] + y_peers + z_peers + x_peers + core_peers
    for peer in peers:
        pl.semaphore_signal(barrier, inc=1, device_id=peer, device_id_type=MESH)
    pl.semaphore_wait(barrier, len(peers))

    def remote(src, dst, send, recv, peer):
        return pltpu.make_async_remote_copy(
            src_ref=src, dst_ref=dst, send_sem=send, recv_sem=recv, device_id=peer, device_id_type=MESH
        )

    vec_halo = [
        remote(vec_hbm, wide.at[pl.ds(0, L)], halo_send.at[0], halo_recv.at[0], right),
        remote(vec_hbm, wide.at[pl.ds(2 * L, L)], halo_send.at[1], halo_recv.at[1], left),
    ]
    for copy in vec_halo:
        copy.start()

    loads[0].wait()
    loads[1].wait()
    loads[2].wait()
    loads[3].wait()

    def coeff_step(ls, acc):
        cs = [dot3(wide[L + l], basis[l], NT) for l in ls]
        for l, c in zip(ls, cs):
            cw[L + l] = pack(c)
        for l, c in zip(ls, cs):
            acc = acc + dot3(c, lt[l], NT)
        return acc

    cluster = groups(coeff_step, jnp.zeros((16, 64), jnp.float32))
    shares[y] = pack(dot3(cluster, ct[0], NT))

    y_copies = [
        remote(shares.at[y], shares.at[y], tree_send.at[n], tree_recv.at[n], peer)
        for n, peer in enumerate(y_peers)
    ]
    for copy in y_copies:
        copy.start()

    coeff_halo = [
        remote(cw.at[pl.ds(L, L)], cw.at[pl.ds(0, L)], halo_send.at[2], halo_recv.at[2], right),
        remote(cw.at[pl.ds(L, L)], cw.at[pl.ds(2 * L, L)], halo_send.at[3], halo_recv.at[3], left),
    ]
    for copy in coeff_halo:
        copy.start()

    loads[5].wait()

    def near_own(ls, carry):
        for l in ls:
            out[l] = dot3(wide[L + l], near[l, 0], NT)
        return carry

    groups(near_own)

    for copy in y_copies:
        copy.wait_recv()
    nodes[core, x, z] = (shares[0] + shares[1]) + (shares[2] + shares[3])
    z_copies = [
        remote(nodes.at[core, x, z], nodes.at[core, x, z], tree_send.at[3 + n], tree_recv.at[3 + n], peer)
        for n, peer in enumerate(z_peers)
    ]
    for copy in z_copies:
        copy.start()
    for copy in z_copies:
        copy.wait_recv()
    x_copies = [
        remote(nodes.at[core, x], nodes.at[core, x], tree_send.at[10 + n], tree_recv.at[10 + n], peer)
        for n, peer in enumerate(x_peers)
    ]
    for copy in x_copies:
        copy.start()
    for copy in x_copies:
        copy.wait_recv()
    core_copies = [
        remote(nodes.at[core], nodes.at[core], tree_send.at[13], tree_recv.at[13], core_peers[0])
    ]
    for copy in core_copies:
        copy.start()
    for copy in core_copies:
        copy.wait_recv()

    loads[4].wait()
    far = jnp.zeros((16, 64), jnp.float32)
    for k in range(16):
        i = branch_index[0, k]
        half = lax.div(i, CS)
        node = nodes[lax.rem(i, CS), lax.div(half, ZS), lax.rem(half, ZS)]
        far = far + dot3(unpack(node), bb[0, k], NT)
    cluster_down = dot3(far, ct[0], NN)

    def down_step(ls, carry):
        for l in ls:
            down[l] = dot3(cluster_down, lt[l], NN)
        return carry

    groups(down_step)

    for copy in vec_halo:
        copy.wait_recv()
    anchor = flat * L - L

    def place(index):
        return jnp.clip(index - anchor, 0, 3 * L - 1)

    def near_step(ls, carry):
        for l in ls:
            acc = out[l]
            for k in (1, 2):
                acc = acc + dot3(wide[place(near_index[k, l])], near[l, k], NT)
            out[l] = acc
        return carry

    groups(near_step)

    for copy in coeff_halo:
        copy.wait_recv()
    loads[6].wait()

    def far_step(ls, carry):
        totals = []
        for l in ls:
            acc = down[l]
            for k in range(4):
                acc = acc + dot3(unpack(cw[place(coup_index[k, l])]), coup[l, k], NT)
            totals.append(acc)
        for l, acc in zip(ls, totals):
            out[l] = out[l] + dot3(acc, basis[l], NN)
        return carry

    groups(far_step)

    for copy in vec_halo + coeff_halo + y_copies + z_copies + x_copies + core_copies:
        copy.wait_send()


def per_device(
    vectors,
    leaf_basis,
    near_index,
    near_blocks,
    coupling_index,
    coupling_blocks,
    leaf_transfer,
    cluster_transfer,
    branch_index,
    branch_blocks,
):
    smem = pl.BlockSpec(memory_space=pltpu.SMEM)
    anywhere = pl.BlockSpec(memory_space=pl.ANY)
    f32 = jnp.float32
    return pl.pallas_call(
        kernel,
        name="h2_product",
        out_shape=jax.ShapeDtypeStruct((L, 16, 128), f32),
        in_specs=[smem] * 3 + [anywhere] * 7,
        out_specs=pl.BlockSpec(memory_space=pltpu.VMEM),
        scratch_shapes=[
            pltpu.VMEM((3 * L, 16, 128), f32),
            pltpu.VMEM((3 * L, 8, 128), f32),
            pltpu.VMEM((L, 64, 128), f32),
            pltpu.VMEM((L, 3, 128, 128), f32),
            pltpu.VMEM((L, 4, 64, 64), f32),
            pltpu.VMEM((L, 64, 64), f32),
            pltpu.VMEM((1, 64, 64), f32),
            pltpu.VMEM((1, 16, 64, 64), f32),
            pltpu.VMEM((YS, 8, 128), f32),
            pltpu.VMEM((CS, XS, ZS, 8, 128), f32),
            pltpu.VMEM((L, 16, 64), f32),
            pltpu.SemaphoreType.DMA((7,)),
            pltpu.SemaphoreType.DMA((4,)),
            pltpu.SemaphoreType.DMA((4,)),
            pltpu.SemaphoreType.DMA((14,)),
            pltpu.SemaphoreType.DMA((14,)),
        ],
        compiler_params=pltpu.CompilerParams(
            collective_id=0, has_side_effects=True, vmem_limit_bytes=56 * 1024 * 1024
        ),
    )(
        near_index.T,
        coupling_index.T,
        branch_index,
        vectors,
        leaf_basis,
        near_blocks,
        coupling_blocks,
        leaf_transfer,
        cluster_transfer,
        branch_blocks,
    )


def solution(mesh):
    rows = ("branch", "sub")
    in_specs = (
        P(rows, None, None),
        P(rows, None, None),
        P(rows, None),
        P(rows, None, None, None),
        P(rows, None),
        P(rows, None, None, None),
        P(rows, None, None),
        P(rows, None, None),
        P("branch", None),
        P("branch", None, None, None),
    )
    return jax.shard_map(
        per_device, mesh=mesh, in_specs=in_specs, out_specs=P(rows, None, None), check_vma=False
    )
```

```python
import jax
import jax.numpy as jnp
from jax import lax
from jax.experimental import pallas as pl
from jax.experimental.pallas import tpu as pltpu
from jax.sharding import PartitionSpec as P

MESH = pl.DeviceIdType.MESH
NT = (((1,), (1,)), ((), ()))
NN = (((1,), (0,)), ((), ()))
XS, ZS, CS, YS = 4, 8, 2, 4
L = 36
CHUNKS = 3
PART = L // CHUNKS
GROUP = 6
F32, BF16 = jnp.float32, jnp.bfloat16


def split(x):
    hi = x.astype(BF16)
    lo = (x - hi.astype(F32)).astype(BF16)
    return hi, lo


def stack(x):
    return jnp.concatenate(split(x), axis=0)


def mm(a, b, dims):
    return lax.dot_general(a, b, dims, preferred_element_type=F32)


def dot3(a, b, dims):
    return dot3_split(a, *split(b), dims)


def dot3_split(a, bh, bl, dims):
    ah, al = split(a)
    rows = a.shape[0]
    both = mm(jnp.concatenate([ah, al], axis=0), bh, dims)
    return both[:rows] + (both[rows:] + mm(ah, bl, dims))


def pack(c):
    return jnp.concatenate([c[:8], c[8:]], axis=1)


def unpack(p):
    return jnp.concatenate([p[:, :64], p[:, 64:]], axis=0)


def groups(body, size=GROUP):
    def step(g, carry):
        body([g * size + i for i in range(size)])
        return carry

    lax.fori_loop(0, L // size, step, 0)


def kernel(
    near_index,
    coup_index,
    branch_index,
    vec_hbm,
    basis_hbm,
    near_hbm,
    coup_hbm,
    lt_hbm,
    ct_hbm,
    bb_hbm,
    out,
    wide,
    cw,
    basis,
    near,
    coup,
    lt,
    ct,
    bb,
    nodes,
    fars,
    bbh,
    bbl,
    down,
    local_sem,
    halo_send,
    halo_recv,
    node_send,
    node_recv,
    far_send,
    far_recv,
    pair_send,
    pair_recv,
):
    b = lax.axis_index("branch")
    y = lax.axis_index("sub")
    core = lax.rem(b, CS)
    z = lax.rem(lax.div(b, CS), ZS)
    x = lax.div(b, CS * ZS)
    flat = b * YS + y
    total = XS * ZS * CS * YS
    right = lax.rem(flat + 1, total)
    left = lax.rem(flat + total - 1, total)
    right = (lax.div(right, YS), lax.rem(right, YS))
    left = (lax.div(left, YS), lax.rem(left, YS))
    mine = x * ZS + z
    slot = core * XS * ZS + mine
    sibling = (b + 1 - 2 * core, y)

    def plane_peer(j):
        px = lax.rem(x + lax.div(j, ZS), XS)
        pz = lax.rem(z + lax.rem(j, ZS), ZS)
        return ((px * ZS + pz) * CS + core, y)

    def row_peer(j):
        return (b, lax.rem(y + j, YS))

    def local(src, dst, n):
        return pltpu.make_async_copy(src, dst, local_sem.at[n])

    first = []
    for i in range(CHUNKS):
        part = pl.ds(i * PART, PART)
        first.append(
            [
                local(vec_hbm.at[part], wide.at[pl.ds(L + i * PART, PART)], 3 * i),
                local(basis_hbm.at[part], basis.at[part], 3 * i + 1),
                local(lt_hbm.at[part], lt.at[part], 3 * i + 2),
            ]
        )
    for loads in first:
        for load in loads:
            load.start()
    n = 3 * CHUNKS
    ct_load = local(ct_hbm, ct, n)
    bb_load = local(bb_hbm, bb, n + 1)
    near_load = local(near_hbm, near, n + 2)
    coup_load = local(coup_hbm, coup, n + 3)
    for load in (ct_load, bb_load, near_load, coup_load):
        load.start()

    barrier = pltpu.get_barrier_semaphore()

    def greet(peer):
        pl.semaphore_signal(barrier, inc=1, device_id=peer, device_id_type=MESH)

    greet(right)
    greet(left)
    greet(sibling)

    def greet_plane(j, carry):
        greet(plane_peer(j))
        return carry

    def greet_row(j, carry):
        greet(row_peer(j))
        return carry

    lax.fori_loop(1, XS * ZS, greet_plane, 0)
    lax.fori_loop(1, YS, greet_row, 0)

    acc = jnp.zeros((32, 128), F32)
    for i in range(CHUNKS):
        for load in first[i]:
            load.wait()
        ls = range(i * PART, (i + 1) * PART)
        cs = [dot3(wide[L + l], basis[l], NT) for l in ls]
        for l, c in zip(ls, cs):
            cw[L + l] = pack(c)
        for l, c in zip(ls, cs):
            acc = acc + mm(stack(c), stack(lt[l]), NT)
    cluster = (acc[:16, :64] + acc[16:, :64]) + (acc[:16, 64:] + acc[16:, 64:])
    ct_load.wait()
    nodes[slot] = pack(dot3(cluster, ct[0], NT))

    pl.semaphore_wait(barrier, 3 + (XS * ZS - 1) + (YS - 1))

    def remote(src, dst, send, recv, peer):
        return pltpu.make_async_remote_copy(
            src_ref=src, dst_ref=dst, send_sem=send, recv_sem=recv, device_id=peer, device_id_type=MESH
        )

    def node_copy(j):
        return remote(
            nodes.at[slot], nodes.at[slot], node_send.at[j], node_recv.at[j], plane_peer(j)
        )

    def far_copy(j):
        return remote(fars.at[y], fars.at[y], far_send.at[j], far_recv.at[j], row_peer(j))

    def pair_copy(j):
        rows = pl.ds((core * XS + lax.rem(x + j, XS)) * ZS, ZS)
        return remote(nodes.at[rows], nodes.at[rows], pair_send.at[j], pair_recv.at[j], sibling)

    def each(lo, hi, body):
        def step(j, carry):
            body(j)
            return carry

        lax.fori_loop(lo, hi, step, 0)

    each(1, XS * ZS, lambda j: node_copy(j).start())

    vec_halo = [
        remote(vec_hbm, wide.at[pl.ds(0, L)], halo_send.at[0], halo_recv.at[0], right),
        remote(vec_hbm, wide.at[pl.ds(2 * L, L)], halo_send.at[1], halo_recv.at[1], left),
    ]
    coeff_halo = [
        remote(cw.at[pl.ds(L, L)], cw.at[pl.ds(0, L)], halo_send.at[2], halo_recv.at[2], right),
        remote(cw.at[pl.ds(L, L)], cw.at[pl.ds(2 * L, L)], halo_send.at[3], halo_recv.at[3], left),
    ]
    for copy in vec_halo + coeff_halo:
        copy.start()

    bb_load.wait()
    for k in range(16):
        bbh[k], bbl[k] = split(bb[0, k])

    def down_step(ls):
        for l in ls:
            step = dot3(dot3(ct[0], lt[l], NN), basis[l], NN)
            hi, lo = split(step)
            down[l, 0:64] = hi
            down[l, 64:128] = hi
            down[l, 128:192] = lo

    groups(down_step)

    near_load.wait()

    def near_own(ls):
        for l in ls:
            out[l] = dot3(wide[L + l], near[l, 0], NT)

    groups(near_own)

    anchor = flat * L - L

    def place(index):
        return jnp.clip(index - anchor, 0, 3 * L - 1)

    for copy in vec_halo:
        copy.wait_recv()

    def near_step(ls):
        for l in ls:
            acc = out[l]
            for k in (1, 2):
                acc = acc + dot3(wide[place(near_index[k, l])], near[l, k], NT)
            out[l] = acc

    groups(near_step)

    for j in (0, 1, 3, 2):
        each(j * ZS + (j == 0), (j + 1) * ZS, lambda n: node_copy(n).wait_recv())
        pair_copy((XS - j) % XS).start()
    each(0, XS, lambda j: pair_copy(j).wait_recv())

    far = jnp.zeros((16, 64), F32)
    for k in range(16):
        i = branch_index[0, k]
        node = nodes[lax.rem(i, CS) * (XS * ZS) + lax.div(i, CS)]
        far = far + dot3_split(unpack(node), bbh[k], bbl[k], NT)
    fars[y] = pack(far)
    each(1, YS, lambda j: far_copy(j).start())

    for copy in coeff_halo:
        copy.wait_recv()
    coup_load.wait()

    def far_step(ls):
        totals = []
        for l in ls:
            acc = jnp.zeros((16, 64), F32)
            for k in range(4):
                acc = acc + dot3(unpack(cw[place(coup_index[k, l])]), coup[l, k], NT)
            totals.append(acc)
        for l, acc in zip(ls, totals):
            out[l] = out[l] + dot3(acc, basis[l], NN)

    groups(far_step)

    each(1, YS, lambda j: far_copy(j).wait_recv())
    far = unpack((fars[0] + fars[1]) + (fars[2] + fars[3]))
    fh, fl = split(far)
    flh = jnp.concatenate([fh, fl, fh], axis=1)
    for l in range(L):
        out[l] = out[l] + mm(flh, down[l], NN)

    for copy in vec_halo + coeff_halo:
        copy.wait_send()
    each(1, XS * ZS, lambda j: node_copy(j).wait_send())
    each(1, YS, lambda j: far_copy(j).wait_send())
    each(0, XS, lambda j: pair_copy(j).wait_send())


def per_device(
    vectors,
    leaf_basis,
    near_index,
    near_blocks,
    coupling_index,
    coupling_blocks,
    leaf_transfer,
    cluster_transfer,
    branch_index,
    branch_blocks,
):
    smem = pl.BlockSpec(memory_space=pltpu.SMEM)
    anywhere = pl.BlockSpec(memory_space=pl.ANY)
    return pl.pallas_call(
        kernel,
        name="h2_product",
        out_shape=jax.ShapeDtypeStruct((L, 16, 128), F32),
        in_specs=[smem] * 3 + [anywhere] * 7,
        out_specs=pl.BlockSpec(memory_space=pltpu.VMEM),
        scratch_shapes=[
            pltpu.VMEM((3 * L, 16, 128), F32),
            pltpu.VMEM((3 * L, 8, 128), F32),
            pltpu.VMEM((L, 64, 128), F32),
            pltpu.VMEM((L, 3, 128, 128), F32),
            pltpu.VMEM((L, 4, 64, 64), F32),
            pltpu.VMEM((L, 64, 64), F32),
            pltpu.VMEM((1, 64, 64), F32),
            pltpu.VMEM((1, 16, 64, 64), F32),
            pltpu.VMEM((CS * XS * ZS, 8, 128), F32),
            pltpu.VMEM((YS, 8, 128), F32),
            pltpu.VMEM((16, 64, 64), BF16),
            pltpu.VMEM((16, 64, 64), BF16),
            pltpu.VMEM((L, 192, 128), BF16),
            pltpu.SemaphoreType.DMA((3 * CHUNKS + 4,)),
            pltpu.SemaphoreType.DMA((4,)),
            pltpu.SemaphoreType.DMA((4,)),
            pltpu.SemaphoreType.DMA((XS * ZS,)),
            pltpu.SemaphoreType.DMA((XS * ZS,)),
            pltpu.SemaphoreType.DMA((YS,)),
            pltpu.SemaphoreType.DMA((YS,)),
            pltpu.SemaphoreType.DMA((XS,)),
            pltpu.SemaphoreType.DMA((XS,)),
        ],
        compiler_params=pltpu.CompilerParams(
            collective_id=0, has_side_effects=True, vmem_limit_bytes=56 * 1024 * 1024
        ),
    )(
        near_index.T,
        coupling_index.T,
        branch_index,
        vectors,
        leaf_basis,
        near_blocks,
        coupling_blocks,
        leaf_transfer,
        cluster_transfer,
        branch_blocks,
    )


def solution(mesh):
    rows = ("branch", "sub")
    in_specs = (
        P(rows, None, None),
        P(rows, None, None),
        P(rows, None),
        P(rows, None, None, None),
        P(rows, None),
        P(rows, None, None, None),
        P(rows, None, None),
        P(rows, None, None),
        P("branch", None),
        P("branch", None, None, None),
    )
    return jax.shard_map(
        per_device, mesh=mesh, in_specs=in_specs, out_specs=P(rows, None, None), check_vma=False
    )
```

```python
import jax
import jax.numpy as jnp
from jax import lax
from jax.experimental import pallas as pl
from jax.experimental.pallas import tpu as pltpu
from jax.sharding import PartitionSpec as P

MESH = pl.DeviceIdType.MESH
NT = (((1,), (1,)), ((), ()))
NN = (((1,), (0,)), ((), ()))
XS, ZS, CS, YS = 4, 8, 2, 4
L = 36
CHUNKS = 3
PART = L // CHUNKS
GROUP = 12
F32, BF16 = jnp.float32, jnp.bfloat16


def split(x):
    hi = x.astype(BF16)
    lo = (x - hi.astype(F32)).astype(BF16)
    return hi, lo


def stack(x):
    return jnp.concatenate(split(x), axis=0)


def mm(a, b, dims):
    return lax.dot_general(a, b, dims, preferred_element_type=F32)


def dot3(a, b, dims):
    return dot3_split(a, *split(b), dims)


def dot3_split(a, bh, bl, dims):
    ah, al = split(a)
    rows = a.shape[0]
    both = mm(jnp.concatenate([ah, al], axis=0), bh, dims)
    return both[:rows] + (both[rows:] + mm(ah, bl, dims))


def pack(c):
    return jnp.concatenate([c[:8], c[8:]], axis=1)


def unpack(p):
    return jnp.concatenate([p[:, :64], p[:, 64:]], axis=0)


def pair(p, q):
    low = lax.broadcasted_iota(jnp.int32, p.shape, 1) < 64
    top = jnp.where(low, p, pltpu.roll(q, 64, 1))
    bottom = jnp.where(low, pltpu.roll(p, 64, 1), q)
    return jnp.concatenate([top, bottom], axis=0)


def fold(s):
    half = s.shape[1] // 2
    both = s[:16] + s[16:]
    return both[:, :half] + both[:, half:]


def wide_split(x):
    hi = x.astype(BF16).astype(F32)
    return jnp.concatenate([hi, x - hi], axis=1).astype(BF16)


def groups(body, size=GROUP):
    def step(g, carry):
        body([g * size + i for i in range(size)])
        return carry

    lax.fori_loop(0, L // size, step, 0)


def kernel(
    near_index,
    coup_index,
    branch_index,
    vec_hbm,
    basis_hbm,
    near_hbm,
    coup_hbm,
    lt_hbm,
    ct_hbm,
    bb_hbm,
    out,
    wide,
    cw,
    basis,
    near,
    coup,
    lt,
    ct,
    bb,
    nodes,
    fars,
    bbh,
    bbl,
    down,
    near12,
    coup4,
    basis2,
    local_sem,
    halo_send,
    halo_recv,
    node_send,
    node_recv,
    far_send,
    far_recv,
    pair_send,
    pair_recv,
):
    b = lax.axis_index("branch")
    y = lax.axis_index("sub")
    core = lax.rem(b, CS)
    z = lax.rem(lax.div(b, CS), ZS)
    x = lax.div(b, CS * ZS)
    flat = b * YS + y
    total = XS * ZS * CS * YS
    right = lax.rem(flat + 1, total)
    left = lax.rem(flat + total - 1, total)
    right = (lax.div(right, YS), lax.rem(right, YS))
    left = (lax.div(left, YS), lax.rem(left, YS))
    mine = x * ZS + z
    slot = core * XS * ZS + mine
    sibling = (b + 1 - 2 * core, y)

    def plane_peer(j):
        px = lax.rem(x + lax.div(j, ZS), XS)
        pz = lax.rem(z + lax.rem(j, ZS), ZS)
        return ((px * ZS + pz) * CS + core, y)

    def row_peer(j):
        return (b, lax.rem(y + j, YS))

    def local(src, dst, n):
        return pltpu.make_async_copy(src, dst, local_sem.at[n])

    first = []
    for i in range(CHUNKS):
        part = pl.ds(i * PART, PART)
        first.append(
            [
                local(vec_hbm.at[part], wide.at[pl.ds(L + i * PART, PART)], 3 * i),
                local(basis_hbm.at[part], basis.at[part], 3 * i + 1),
                local(lt_hbm.at[part], lt.at[part], 3 * i + 2),
            ]
        )
    for loads in first:
        for load in loads:
            load.start()
    n = 3 * CHUNKS
    ct_load = local(ct_hbm, ct, n)
    bb_load = local(bb_hbm, bb, n + 1)
    near_load = local(near_hbm, near, n + 2)
    coup_load = local(coup_hbm, coup, n + 3)
    for load in (ct_load, bb_load, near_load, coup_load):
        load.start()

    barrier = pltpu.get_barrier_semaphore()

    def greet(peer):
        pl.semaphore_signal(barrier, inc=1, device_id=peer, device_id_type=MESH)

    greet(right)
    greet(left)
    greet(sibling)

    def greet_plane(j, carry):
        greet(plane_peer(j))
        return carry

    def greet_row(j, carry):
        greet(row_peer(j))
        return carry

    lax.fori_loop(1, XS * ZS, greet_plane, 0)
    lax.fori_loop(1, YS, greet_row, 0)

    acc = jnp.zeros((32, 128), F32)
    for i in range(CHUNKS):
        for load in first[i]:
            load.wait()
        ls = range(i * PART, (i + 1) * PART)
        cs = [dot3(wide[L + l], basis[l], NT) for l in ls]
        for l, c in zip(ls, cs):
            cw[L + l] = pack(c)
        for l, c in zip(ls, cs):
            acc = acc + mm(stack(c), stack(lt[l]), NT)
    cluster = (acc[:16, :64] + acc[16:, :64]) + (acc[:16, 64:] + acc[16:, 64:])
    ct_load.wait()
    nodes[slot] = pack(dot3(cluster, ct[0], NT))

    pl.semaphore_wait(barrier, 3 + (XS * ZS - 1) + (YS - 1))

    def remote(src, dst, send, recv, peer):
        return pltpu.make_async_remote_copy(
            src_ref=src, dst_ref=dst, send_sem=send, recv_sem=recv, device_id=peer, device_id_type=MESH
        )

    def node_copy(j):
        return remote(
            nodes.at[slot], nodes.at[slot], node_send.at[j], node_recv.at[j], plane_peer(j)
        )

    def far_copy(j):
        return remote(fars.at[y], fars.at[y], far_send.at[j], far_recv.at[j], row_peer(j))

    def pair_copy(j):
        rows = pl.ds((core * XS + lax.rem(x + j, XS)) * ZS, ZS)
        return remote(nodes.at[rows], nodes.at[rows], pair_send.at[j], pair_recv.at[j], sibling)

    def each(lo, hi, body):
        def step(j, carry):
            body(j)
            return carry

        lax.fori_loop(lo, hi, step, 0)

    vec_halo = [
        remote(vec_hbm, wide.at[pl.ds(0, L)], halo_send.at[0], halo_recv.at[0], right),
        remote(vec_hbm, wide.at[pl.ds(2 * L, L)], halo_send.at[1], halo_recv.at[1], left),
    ]
    coeff_halo = [
        remote(cw.at[pl.ds(L, L)], cw.at[pl.ds(0, L)], halo_send.at[2], halo_recv.at[2], right),
        remote(cw.at[pl.ds(L, L)], cw.at[pl.ds(2 * L, L)], halo_send.at[3], halo_recv.at[3], left),
    ]
    early = z < ZS // 2

    def start_halos():
        for copy in vec_halo + coeff_halo:
            copy.start()

    pl.when(early)(start_halos)
    each(1, XS * ZS, lambda j: node_copy(j).start())
    pl.when(jnp.logical_not(early))(start_halos)

    bb_load.wait()
    for k in range(16):
        bbh[k], bbl[k] = split(bb[0, k])

    def down_step(ls):
        for l in ls:
            step = dot3(dot3(ct[0], lt[l], NN), basis[l], NN)
            hi, lo = split(step)
            down[l, 0:64] = hi
            down[l, 64:128] = hi
            down[l, 128:192] = lo

    groups(down_step)

    near_load.wait()

    def near_own(ls):
        for l in ls:
            out[l] = dot3(wide[L + l], near[l, 0], NT)
        for l in ls:
            for k in (1, 2):
                near12[l, (k - 1) * 128 : k * 128] = wide_split(near[l, k].T)

    groups(near_own)

    coup_load.wait()

    def coup_own(ls):
        for l in ls:
            for k in range(4):
                coup4[l, k * 64 : (k + 1) * 64] = wide_split(coup[l, k].T)
            basis2[l] = wide_split(basis[l])

    groups(coup_own)

    anchor = flat * L - L

    def place(index):
        return jnp.clip(index - anchor, 0, 3 * L - 1)

    for copy in vec_halo:
        copy.wait_recv()

    def near_step(ls):
        for l in ls:
            h1, l1 = split(wide[place(near_index[1, l])])
            h2, l2 = split(wide[place(near_index[2, l])])
            rows = jnp.concatenate(
                [jnp.concatenate([h1, h2], axis=1), jnp.concatenate([l1, l2], axis=1)], axis=0
            )
            out[l] = out[l] + fold(mm(rows, near12[l], NN))

    groups(near_step)

    for j in (0, 1, 3, 2):
        each(j * ZS + (j == 0), (j + 1) * ZS, lambda n: node_copy(n).wait_recv())
        pair_copy((XS - j) % XS).start()
    each(0, XS, lambda j: pair_copy(j).wait_recv())

    far = jnp.zeros((16, 64), F32)
    for k in range(16):
        i = branch_index[0, k]
        node = nodes[lax.rem(i, CS) * (XS * ZS) + lax.div(i, CS)]
        far = far + dot3_split(unpack(node), bbh[k], bbl[k], NT)
    fars[y] = pack(far)
    each(1, YS, lambda j: far_copy(j).start())

    for copy in coeff_halo:
        copy.wait_recv()

    def far_step(ls):
        totals = []
        for l in ls:
            p = [cw[place(coup_index[k, l])] for k in range(4)]
            rows = stack(jnp.concatenate([pair(p[0], p[1]), pair(p[2], p[3])], axis=1))
            totals.append(fold(mm(rows, coup4[l], NN)))
        for l, acc in zip(ls, totals):
            out[l] = out[l] + fold(mm(stack(acc), basis2[l], NN))

    groups(far_step)

    each(1, YS, lambda j: far_copy(j).wait_recv())
    far = unpack((fars[0] + fars[1]) + (fars[2] + fars[3]))
    fh, fl = split(far)
    flh = jnp.concatenate([fh, fl, fh], axis=1)
    for l in range(L):
        out[l] = out[l] + mm(flh, down[l], NN)

    for copy in vec_halo + coeff_halo:
        copy.wait_send()
    each(1, XS * ZS, lambda j: node_copy(j).wait_send())
    each(1, YS, lambda j: far_copy(j).wait_send())
    each(0, XS, lambda j: pair_copy(j).wait_send())


def per_device(
    vectors,
    leaf_basis,
    near_index,
    near_blocks,
    coupling_index,
    coupling_blocks,
    leaf_transfer,
    cluster_transfer,
    branch_index,
    branch_blocks,
):
    smem = pl.BlockSpec(memory_space=pltpu.SMEM)
    anywhere = pl.BlockSpec(memory_space=pl.ANY)
    return pl.pallas_call(
        kernel,
        name="h2_product",
        out_shape=jax.ShapeDtypeStruct((L, 16, 128), F32),
        in_specs=[smem] * 3 + [anywhere] * 7,
        out_specs=pl.BlockSpec(memory_space=pltpu.VMEM),
        scratch_shapes=[
            pltpu.VMEM((3 * L, 16, 128), F32),
            pltpu.VMEM((3 * L, 8, 128), F32),
            pltpu.VMEM((L, 64, 128), F32),
            pltpu.VMEM((L, 3, 128, 128), F32),
            pltpu.VMEM((L, 4, 64, 64), F32),
            pltpu.VMEM((L, 64, 64), F32),
            pltpu.VMEM((1, 64, 64), F32),
            pltpu.VMEM((1, 16, 64, 64), F32),
            pltpu.VMEM((CS * XS * ZS, 8, 128), F32),
            pltpu.VMEM((YS, 8, 128), F32),
            pltpu.VMEM((16, 64, 64), BF16),
            pltpu.VMEM((16, 64, 64), BF16),
            pltpu.VMEM((L, 192, 128), BF16),
            pltpu.VMEM((L, 256, 256), BF16),
            pltpu.VMEM((L, 256, 128), BF16),
            pltpu.VMEM((L, 64, 256), BF16),
            pltpu.SemaphoreType.DMA((3 * CHUNKS + 4,)),
            pltpu.SemaphoreType.DMA((4,)),
            pltpu.SemaphoreType.DMA((4,)),
            pltpu.SemaphoreType.DMA((XS * ZS,)),
            pltpu.SemaphoreType.DMA((XS * ZS,)),
            pltpu.SemaphoreType.DMA((YS,)),
            pltpu.SemaphoreType.DMA((YS,)),
            pltpu.SemaphoreType.DMA((XS,)),
            pltpu.SemaphoreType.DMA((XS,)),
        ],
        compiler_params=pltpu.CompilerParams(
            collective_id=0, has_side_effects=True, vmem_limit_bytes=56 * 1024 * 1024
        ),
    )(
        near_index.T,
        coupling_index.T,
        branch_index,
        vectors,
        leaf_basis,
        near_blocks,
        coupling_blocks,
        leaf_transfer,
        cluster_transfer,
        branch_blocks,
    )


def solution(mesh):
    rows = ("branch", "sub")
    in_specs = (
        P(rows, None, None),
        P(rows, None, None),
        P(rows, None),
        P(rows, None, None, None),
        P(rows, None),
        P(rows, None, None, None),
        P(rows, None, None),
        P(rows, None, None),
        P("branch", None),
        P("branch", None, None, None),
    )
    return jax.shard_map(
        per_device, mesh=mesh, in_specs=in_specs, out_specs=P(rows, None, None), check_vma=False
    )
```

```python
import jax
import jax.numpy as jnp
from jax import lax
from jax.experimental import pallas as pl
from jax.experimental.pallas import tpu as pltpu
from jax.sharding import PartitionSpec as P

MESH = pl.DeviceIdType.MESH
NT = (((1,), (1,)), ((), ()))
NN = (((1,), (0,)), ((), ()))
XS, ZS, CS, YS = 4, 8, 2, 4
L = 36
CHUNKS = 3
PART = L // CHUNKS
GROUP = 12
F32, BF16 = jnp.float32, jnp.bfloat16


def split(x):
    hi = x.astype(BF16)
    lo = (x - hi.astype(F32)).astype(BF16)
    return hi, lo


def stack(x):
    return jnp.concatenate(split(x), axis=0)


def mm(a, b, dims):
    return lax.dot_general(a, b, dims, preferred_element_type=F32)


def dot3(a, b, dims):
    return dot3_split(a, *split(b), dims)


def dot3_split(a, bh, bl, dims):
    ah, al = split(a)
    rows = a.shape[0]
    both = mm(jnp.concatenate([ah, al], axis=0), bh, dims)
    return both[:rows] + (both[rows:] + mm(ah, bl, dims))


def pack(c):
    return jnp.concatenate([c[:8], c[8:]], axis=1)


def unpack(p):
    return jnp.concatenate([p[:, :64], p[:, 64:]], axis=0)


def pair(p, q):
    low = lax.broadcasted_iota(jnp.int32, p.shape, 1) < 64
    top = jnp.where(low, p, pltpu.roll(q, 64, 1))
    bottom = jnp.where(low, pltpu.roll(p, 64, 1), q)
    return jnp.concatenate([top, bottom], axis=0)


def fold(s):
    half = s.shape[1] // 2
    both = s[:16] + s[16:]
    return both[:, :half] + both[:, half:]


def wide_split(x):
    hi = x.astype(BF16).astype(F32)
    return jnp.concatenate([hi, x - hi], axis=1).astype(BF16)


def groups(body, size=GROUP):
    def step(g, carry):
        body([g * size + i for i in range(size)])
        return carry

    lax.fori_loop(0, L // size, step, 0)


def kernel(
    near_index,
    coup_index,
    branch_index,
    vec_hbm,
    basis_hbm,
    near_hbm,
    coup_hbm,
    lt_hbm,
    ct_hbm,
    bb_hbm,
    out,
    wide,
    cw,
    basis,
    near,
    coup,
    lt,
    ct,
    bb,
    nodes,
    fars,
    bbh,
    bbl,
    down,
    near12,
    coup4,
    basis2,
    local_sem,
    halo_send,
    halo_recv,
    node_send,
    node_recv,
    far_send,
    far_recv,
    pair_send,
    pair_recv,
):
    b = lax.axis_index("branch")
    y = lax.axis_index("sub")
    core = lax.rem(b, CS)
    z = lax.rem(lax.div(b, CS), ZS)
    x = lax.div(b, CS * ZS)
    flat = b * YS + y
    total = XS * ZS * CS * YS
    right = lax.rem(flat + 1, total)
    left = lax.rem(flat + total - 1, total)
    right = (lax.div(right, YS), lax.rem(right, YS))
    left = (lax.div(left, YS), lax.rem(left, YS))
    mine = x * ZS + z
    slot = core * XS * ZS + mine
    sibling = (b + 1 - 2 * core, y)

    def plane_peer(j):
        px = lax.rem(x + lax.div(j, ZS), XS)
        pz = lax.rem(z + lax.rem(j, ZS), ZS)
        return ((px * ZS + pz) * CS + core, y)

    def row_peer(j):
        return (b, lax.rem(y + j, YS))

    def local(src, dst, n):
        return pltpu.make_async_copy(src, dst, local_sem.at[n])

    first = []
    for i in range(CHUNKS):
        part = pl.ds(i * PART, PART)
        first.append(
            [
                local(vec_hbm.at[part], wide.at[pl.ds(L + i * PART, PART)], 3 * i),
                local(basis_hbm.at[part], basis.at[part], 3 * i + 1),
                local(lt_hbm.at[part], lt.at[part], 3 * i + 2),
            ]
        )
    for loads in first:
        for load in loads:
            load.start()
    n = 3 * CHUNKS
    ct_load = local(ct_hbm, ct, n)
    bb_load = local(bb_hbm, bb, n + 1)
    near_load = local(near_hbm, near, n + 2)
    coup_load = local(coup_hbm, coup, n + 3)
    for load in (ct_load, bb_load, near_load, coup_load):
        load.start()

    barrier = pltpu.get_barrier_semaphore()

    def greet(peer):
        pl.semaphore_signal(barrier, inc=1, device_id=peer, device_id_type=MESH)

    greet(right)
    greet(left)
    greet(sibling)

    def greet_plane(j, carry):
        greet(plane_peer(j))
        return carry

    def greet_row(j, carry):
        greet(row_peer(j))
        return carry

    lax.fori_loop(1, XS * ZS, greet_plane, 0)
    lax.fori_loop(1, YS, greet_row, 0)

    acc = jnp.zeros((32, 128), F32)
    for i in range(CHUNKS):
        for load in first[i]:
            load.wait()
        ls = range(i * PART, (i + 1) * PART)
        cs = [dot3(wide[L + l], basis[l], NT) for l in ls]
        for l, c in zip(ls, cs):
            cw[L + l] = pack(c)
        for l, c in zip(ls, cs):
            acc = acc + mm(stack(c), stack(lt[l]), NT)
    cluster = (acc[:16, :64] + acc[16:, :64]) + (acc[:16, 64:] + acc[16:, 64:])
    ct_load.wait()
    nodes[slot] = pack(dot3(cluster, ct[0], NT))

    pl.semaphore_wait(barrier, 3 + (XS * ZS - 1) + (YS - 1))

    def remote(src, dst, send, recv, peer):
        return pltpu.make_async_remote_copy(
            src_ref=src, dst_ref=dst, send_sem=send, recv_sem=recv, device_id=peer, device_id_type=MESH
        )

    def node_copy(j):
        return remote(
            nodes.at[slot], nodes.at[slot], node_send.at[j], node_recv.at[j], plane_peer(j)
        )

    def far_copy(j):
        return remote(fars.at[y], fars.at[y], far_send.at[j], far_recv.at[j], row_peer(j))

    def pair_copy(j):
        rows = pl.ds((core * XS + lax.rem(x + j, XS)) * ZS, ZS)
        return remote(nodes.at[rows], nodes.at[rows], pair_send.at[j], pair_recv.at[j], sibling)

    def each(lo, hi, body):
        def step(j, carry):
            body(j)
            return carry

        lax.fori_loop(lo, hi, step, 0)

    vec_halo = [
        remote(vec_hbm, wide.at[pl.ds(0, L)], halo_send.at[0], halo_recv.at[0], right),
        remote(vec_hbm, wide.at[pl.ds(2 * L, L)], halo_send.at[1], halo_recv.at[1], left),
    ]
    coeff_halo = [
        remote(cw.at[pl.ds(L, L)], cw.at[pl.ds(0, L)], halo_send.at[2], halo_recv.at[2], right),
        remote(cw.at[pl.ds(L, L)], cw.at[pl.ds(2 * L, L)], halo_send.at[3], halo_recv.at[3], left),
    ]
    early = z < ZS // 2

    def start_halos():
        for copy in vec_halo + coeff_halo:
            copy.start()

    pl.when(early)(start_halos)
    each(1, XS * ZS, lambda j: node_copy(j).start())
    pl.when(jnp.logical_not(early))(start_halos)

    bb_load.wait()
    for k in range(16):
        bbh[k], bbl[k] = split(bb[0, k])

    def down_step(ls):
        for l in ls:
            step = dot3(dot3(ct[0], lt[l], NN), basis[l], NN)
            hi, lo = split(step)
            down[l, 0:64] = hi
            down[l, 64:128] = hi
            down[l, 128:192] = lo

    groups(down_step)

    near_load.wait()

    def near_own(ls):
        for l in ls:
            out[l] = dot3(wide[L + l], near[l, 0], NT)
        for l in ls:
            for k in (1, 2):
                near12[l, (k - 1) * 128 : k * 128] = wide_split(near[l, k].T)

    groups(near_own)

    coup_load.wait()

    def coup_own(ls):
        for l in ls:
            for k in range(4):
                coup4[l, k * 64 : (k + 1) * 64] = wide_split(coup[l, k].T)
            basis2[l] = wide_split(basis[l])

    groups(coup_own)

    anchor = flat * L - L

    def place(index):
        return jnp.clip(index - anchor, 0, 3 * L - 1)

    for copy in vec_halo:
        copy.wait_recv()

    def near_step(ls):
        for l in ls:
            h1, l1 = split(wide[place(near_index[1, l])])
            h2, l2 = split(wide[place(near_index[2, l])])
            rows = jnp.concatenate(
                [jnp.concatenate([h1, h2], axis=1), jnp.concatenate([l1, l2], axis=1)], axis=0
            )
            out[l] = out[l] + fold(mm(rows, near12[l], NN))

    groups(near_step, 18)

    for j in (0, 1, 3, 2):
        each(j * ZS + (j == 0), (j + 1) * ZS, lambda n: node_copy(n).wait_recv())
        pair_copy((XS - j) % XS).start()
    each(0, XS, lambda j: pair_copy(j).wait_recv())

    far = jnp.zeros((16, 64), F32)
    for k in range(16):
        i = branch_index[0, k]
        node = nodes[lax.rem(i, CS) * (XS * ZS) + lax.div(i, CS)]
        far = far + dot3_split(unpack(node), bbh[k], bbl[k], NT)
    fars[y] = pack(far)
    each(1, YS, lambda j: far_copy(j).start())

    for copy in coeff_halo:
        copy.wait_recv()

    def far_step(ls):
        totals = []
        for l in ls:
            p = [cw[place(coup_index[k, l])] for k in range(4)]
            rows = stack(jnp.concatenate([pair(p[0], p[1]), pair(p[2], p[3])], axis=1))
            totals.append(fold(mm(rows, coup4[l], NN)))
        for l, acc in zip(ls, totals):
            out[l] = out[l] + fold(mm(stack(acc), basis2[l], NN))

    groups(far_step, 18)

    each(1, YS, lambda j: far_copy(j).wait_recv())
    far = unpack((fars[0] + fars[1]) + (fars[2] + fars[3]))
    fh, fl = split(far)
    flh = jnp.concatenate([fh, fl, fh], axis=1)
    for l in range(L):
        out[l] = out[l] + mm(flh, down[l], NN)

    for copy in vec_halo + coeff_halo:
        copy.wait_send()
    each(1, XS * ZS, lambda j: node_copy(j).wait_send())
    each(1, YS, lambda j: far_copy(j).wait_send())
    each(0, XS, lambda j: pair_copy(j).wait_send())


def store(source, target, sem):
    copy = pltpu.make_async_copy(source, target, sem)
    copy.start()
    copy.wait()


def per_device(
    vectors,
    leaf_basis,
    near_index,
    near_blocks,
    coupling_index,
    coupling_blocks,
    leaf_transfer,
    cluster_transfer,
    branch_index,
    branch_blocks,
):
    smem = pl.BlockSpec(memory_space=pltpu.SMEM)
    anywhere = pl.BlockSpec(memory_space=pl.ANY)
    result = pl.pallas_call(
        kernel,
        name="h2_product",
        out_shape=pltpu.VMEM((L, 16, 128), F32),
        in_specs=[smem] * 3 + [anywhere] * 7,
        out_specs=pl.BlockSpec(memory_space=pltpu.VMEM),
        scratch_shapes=[
            pltpu.VMEM((3 * L, 16, 128), F32),
            pltpu.VMEM((3 * L, 8, 128), F32),
            pltpu.VMEM((L, 64, 128), F32),
            pltpu.VMEM((L, 3, 128, 128), F32),
            pltpu.VMEM((L, 4, 64, 64), F32),
            pltpu.VMEM((L, 64, 64), F32),
            pltpu.VMEM((1, 64, 64), F32),
            pltpu.VMEM((1, 16, 64, 64), F32),
            pltpu.VMEM((CS * XS * ZS, 8, 128), F32),
            pltpu.VMEM((YS, 8, 128), F32),
            pltpu.VMEM((16, 64, 64), BF16),
            pltpu.VMEM((16, 64, 64), BF16),
            pltpu.VMEM((L, 192, 128), BF16),
            pltpu.VMEM((L, 256, 256), BF16),
            pltpu.VMEM((L, 256, 128), BF16),
            pltpu.VMEM((L, 64, 256), BF16),
            pltpu.SemaphoreType.DMA((3 * CHUNKS + 4,)),
            pltpu.SemaphoreType.DMA((4,)),
            pltpu.SemaphoreType.DMA((4,)),
            pltpu.SemaphoreType.DMA((XS * ZS,)),
            pltpu.SemaphoreType.DMA((XS * ZS,)),
            pltpu.SemaphoreType.DMA((YS,)),
            pltpu.SemaphoreType.DMA((YS,)),
            pltpu.SemaphoreType.DMA((XS,)),
            pltpu.SemaphoreType.DMA((XS,)),
        ],
        compiler_params=pltpu.CompilerParams(
            collective_id=0, has_side_effects=True, vmem_limit_bytes=56 * 1024 * 1024
        ),
    )(
        near_index.T,
        coupling_index.T,
        branch_index,
        vectors,
        leaf_basis,
        near_blocks,
        coupling_blocks,
        leaf_transfer,
        cluster_transfer,
        branch_blocks,
    )
    result = pltpu.with_memory_space_constraint(result, pltpu.VMEM)
    return pl.pallas_call(
        store,
        name="store",
        out_shape=jax.ShapeDtypeStruct((L, 16, 128), F32),
        in_specs=[pl.BlockSpec(memory_space=pltpu.VMEM)],
        out_specs=anywhere,
        scratch_shapes=[pltpu.SemaphoreType.DMA],
    )(result)


def solution(mesh):
    rows = ("branch", "sub")
    in_specs = (
        P(rows, None, None),
        P(rows, None, None),
        P(rows, None),
        P(rows, None, None, None),
        P(rows, None),
        P(rows, None, None, None),
        P(rows, None, None),
        P(rows, None, None),
        P("branch", None),
        P("branch", None, None, None),
    )
    return jax.shard_map(
        per_device, mesh=mesh, in_specs=in_specs, out_specs=P(rows, None, None), check_vma=False
    )
```

```python
import jax
import jax.numpy as jnp
from jax import lax
from jax.experimental import pallas as pl
from jax.experimental.pallas import tpu as pltpu
from jax.sharding import PartitionSpec as P

MESH = pl.DeviceIdType.MESH
NT = (((1,), (1,)), ((), ()))
NN = (((1,), (0,)), ((), ()))
XS, ZS, CS, YS = 4, 8, 2, 4
L = 36
CHUNKS = 3
PART = L // CHUNKS
GROUP = 12
F32, BF16 = jnp.float32, jnp.bfloat16


def split(x):
    hi = x.astype(BF16)
    lo = (x - hi.astype(F32)).astype(BF16)
    return hi, lo


def stack(x):
    return jnp.concatenate(split(x), axis=0)


def mm(a, b, dims):
    return lax.dot_general(a, b, dims, preferred_element_type=F32)


def dot3(a, b, dims):
    return dot3_split(a, *split(b), dims)


def dot3_split(a, bh, bl, dims):
    ah, al = split(a)
    rows = a.shape[0]
    both = mm(jnp.concatenate([ah, al], axis=0), bh, dims)
    return both[:rows] + (both[rows:] + mm(ah, bl, dims))


def pack(c):
    return jnp.concatenate([c[:8], c[8:]], axis=1)


def unpack(p):
    return jnp.concatenate([p[:, :64], p[:, 64:]], axis=0)


def pair(p, q):
    low = lax.broadcasted_iota(jnp.int32, p.shape, 1) < 64
    top = jnp.where(low, p, pltpu.roll(q, 64, 1))
    bottom = jnp.where(low, pltpu.roll(p, 64, 1), q)
    return jnp.concatenate([top, bottom], axis=0)


def fold(s):
    half = s.shape[1] // 2
    both = s[:16] + s[16:]
    return both[:, :half] + both[:, half:]


def wide_split(x):
    hi = x.astype(BF16).astype(F32)
    return jnp.concatenate([hi, x - hi], axis=1).astype(BF16)


def groups(body, size=GROUP):
    def step(g, carry):
        body([g * size + i for i in range(size)])
        return carry

    lax.fori_loop(0, L // size, step, 0)


def kernel(
    near_index,
    coup_index,
    branch_index,
    vec_hbm,
    basis_hbm,
    near_hbm,
    coup_hbm,
    lt_hbm,
    ct_hbm,
    bb_hbm,
    out,
    wide,
    cw,
    basis,
    near,
    coup,
    lt,
    ct,
    bb,
    nodes,
    fars,
    bbh,
    bbl,
    down,
    near12,
    coup4,
    basis2,
    local_sem,
    halo_send,
    halo_recv,
    node_send,
    node_recv,
    far_send,
    far_recv,
    pair_send,
    pair_recv,
):
    b = lax.axis_index("branch")
    y = lax.axis_index("sub")
    core = lax.rem(b, CS)
    z = lax.rem(lax.div(b, CS), ZS)
    x = lax.div(b, CS * ZS)
    flat = b * YS + y
    total = XS * ZS * CS * YS
    right = lax.rem(flat + 1, total)
    left = lax.rem(flat + total - 1, total)
    right = (lax.div(right, YS), lax.rem(right, YS))
    left = (lax.div(left, YS), lax.rem(left, YS))
    mine = x * ZS + z
    slot = core * XS * ZS + mine
    sibling = (b + 1 - 2 * core, y)

    def plane_peer(j):
        px = lax.rem(x + lax.div(j, ZS), XS)
        pz = lax.rem(z + lax.rem(j, ZS), ZS)
        return ((px * ZS + pz) * CS + core, y)

    def far_first(n):
        q = lax.div(n, XS)
        sign = 1 - 2 * lax.rem(q, 2)
        dz = lax.rem(ZS // 2 + sign * lax.div(q + 1, 2) + ZS, ZS)
        return (XS - 1 - lax.rem(n, XS)) * ZS + dz

    def row_peer(j):
        return (b, lax.rem(y + j, YS))

    def local(src, dst, n):
        return pltpu.make_async_copy(src, dst, local_sem.at[n])

    barrier = pltpu.get_barrier_semaphore()

    def greet(peer):
        pl.semaphore_signal(barrier, inc=1, device_id=peer, device_id_type=MESH)


    def greet_plane(n, carry):
        greet(plane_peer(far_first(n)))
        return carry

    def greet_row(j, carry):
        greet(row_peer(j))
        return carry

    lax.fori_loop(0, XS * ZS - 1, greet_plane, 0)
    greet(right)
    greet(left)
    greet(sibling)
    lax.fori_loop(1, YS, greet_row, 0)

    first = []
    for i in range(CHUNKS):
        part = pl.ds(i * PART, PART)
        first.append(
            [
                local(vec_hbm.at[part], wide.at[pl.ds(L + i * PART, PART)], 3 * i),
                local(basis_hbm.at[part], basis.at[part], 3 * i + 1),
                local(lt_hbm.at[part], lt.at[part], 3 * i + 2),
            ]
        )
    for loads in first:
        for load in loads:
            load.start()
    n = 3 * CHUNKS
    ct_load = local(ct_hbm, ct, n)
    bb_load = local(bb_hbm, bb, n + 1)
    near_load = local(near_hbm, near, n + 2)
    coup_load = local(coup_hbm, coup, n + 3)
    for load in (ct_load, bb_load, near_load, coup_load):
        load.start()

    acc = jnp.zeros((32, 128), F32)
    for i in range(CHUNKS):
        for load in first[i]:
            load.wait()
        ls = range(i * PART, (i + 1) * PART)
        cs = [dot3(wide[L + l], basis[l], NT) for l in ls]
        for l, c in zip(ls, cs):
            cw[L + l] = pack(c)
        for l, c in zip(ls, cs):
            acc = acc + mm(stack(c), stack(lt[l]), NT)
    cluster = (acc[:16, :64] + acc[16:, :64]) + (acc[:16, 64:] + acc[16:, 64:])
    ct_load.wait()
    nodes[slot] = pack(dot3(cluster, ct[0], NT))

    pl.semaphore_wait(barrier, 3 + (XS * ZS - 1) + (YS - 1))

    def remote(src, dst, send, recv, peer):
        return pltpu.make_async_remote_copy(
            src_ref=src, dst_ref=dst, send_sem=send, recv_sem=recv, device_id=peer, device_id_type=MESH
        )

    def node_copy(j):
        return remote(
            nodes.at[slot], nodes.at[slot], node_send.at[j], node_recv.at[j], plane_peer(j)
        )

    def far_copy(j):
        return remote(fars.at[y], fars.at[y], far_send.at[j], far_recv.at[j], row_peer(j))

    def pair_copy(j):
        rows = pl.ds((core * XS + lax.rem(x + j, XS)) * ZS, ZS)
        return remote(nodes.at[rows], nodes.at[rows], pair_send.at[j], pair_recv.at[j], sibling)

    def each(lo, hi, body):
        def step(j, carry):
            body(j)
            return carry

        lax.fori_loop(lo, hi, step, 0)

    vec_halo = [
        remote(vec_hbm, wide.at[pl.ds(0, L)], halo_send.at[0], halo_recv.at[0], right),
        remote(vec_hbm, wide.at[pl.ds(2 * L, L)], halo_send.at[1], halo_recv.at[1], left),
    ]
    coeff_halo = [
        remote(cw.at[pl.ds(L, L)], cw.at[pl.ds(0, L)], halo_send.at[2], halo_recv.at[2], right),
        remote(cw.at[pl.ds(L, L)], cw.at[pl.ds(2 * L, L)], halo_send.at[3], halo_recv.at[3], left),
    ]
    early = z < ZS // 2

    def start_halos():
        for copy in coeff_halo + vec_halo:
            copy.start()

    pl.when(early)(start_halos)
    each(0, XS * ZS - 1, lambda n: node_copy(far_first(n)).start())
    pl.when(jnp.logical_not(early))(start_halos)

    bb_load.wait()
    for k in range(16):
        bbh[k], bbl[k] = split(bb[0, k])

    def down_step(ls):
        for l in ls:
            step = dot3(dot3(ct[0], lt[l], NN), basis[l], NN)
            hi, lo = split(step)
            down[l, 0:64] = hi
            down[l, 64:128] = hi
            down[l, 128:192] = lo

    groups(down_step)

    near_load.wait()

    def near_own(ls):
        for l in ls:
            out[l] = dot3(wide[L + l], near[l, 0], NT)
        for l in ls:
            for k in (1, 2):
                near12[l, (k - 1) * 128 : k * 128] = wide_split(near[l, k].T)

    groups(near_own)

    coup_load.wait()

    def coup_own(ls):
        for l in ls:
            for k in range(4):
                coup4[l, k * 64 : (k + 1) * 64] = wide_split(coup[l, k].T)
            basis2[l] = wide_split(basis[l])

    groups(coup_own)

    anchor = flat * L - L

    def place(index):
        return jnp.clip(index - anchor, 0, 3 * L - 1)

    for copy in coeff_halo:
        copy.wait_recv()

    def far_step(ls):
        totals = []
        for l in ls:
            p = [cw[place(coup_index[k, l])] for k in range(4)]
            rows = stack(jnp.concatenate([pair(p[0], p[1]), pair(p[2], p[3])], axis=1))
            totals.append(fold(mm(rows, coup4[l], NN)))
        for l, acc in zip(ls, totals):
            out[l] = out[l] + fold(mm(stack(acc), basis2[l], NN))

    groups(far_step, 18)

    for j in (0, 1, 3, 2):
        each(j * ZS + (j == 0), (j + 1) * ZS, lambda n: node_copy(n).wait_recv())
        pair_copy((XS - j) % XS).start()
    each(0, XS, lambda j: pair_copy(j).wait_recv())

    far = jnp.zeros((16, 64), F32)
    for k in range(16):
        i = branch_index[0, k]
        node = nodes[lax.rem(i, CS) * (XS * ZS) + lax.div(i, CS)]
        far = far + dot3_split(unpack(node), bbh[k], bbl[k], NT)
    fars[y] = pack(far)
    each(1, YS, lambda j: far_copy(j).start())

    for copy in vec_halo:
        copy.wait_recv()

    def near_step(ls):
        for l in ls:
            h1, l1 = split(wide[place(near_index[1, l])])
            h2, l2 = split(wide[place(near_index[2, l])])
            rows = jnp.concatenate(
                [jnp.concatenate([h1, h2], axis=1), jnp.concatenate([l1, l2], axis=1)], axis=0
            )
            out[l] = out[l] + fold(mm(rows, near12[l], NN))

    groups(near_step, 18)

    each(1, YS, lambda j: far_copy(j).wait_recv())
    far = unpack((fars[0] + fars[1]) + (fars[2] + fars[3]))
    fh, fl = split(far)
    flh = jnp.concatenate([fh, fl, fh], axis=1)
    for l in range(L):
        out[l] = out[l] + mm(flh, down[l], NN)

    for copy in vec_halo + coeff_halo:
        copy.wait_send()
    each(1, XS * ZS, lambda j: node_copy(j).wait_send())
    each(1, YS, lambda j: far_copy(j).wait_send())
    each(0, XS, lambda j: pair_copy(j).wait_send())


def store(source, target, sem):
    copy = pltpu.make_async_copy(source, target, sem)
    copy.start()
    copy.wait()


def per_device(
    vectors,
    leaf_basis,
    near_index,
    near_blocks,
    coupling_index,
    coupling_blocks,
    leaf_transfer,
    cluster_transfer,
    branch_index,
    branch_blocks,
):
    smem = pl.BlockSpec(memory_space=pltpu.SMEM)
    anywhere = pl.BlockSpec(memory_space=pl.ANY)
    result = pl.pallas_call(
        kernel,
        name="h2_product",
        out_shape=pltpu.VMEM((L, 16, 128), F32),
        in_specs=[smem] * 3 + [anywhere] * 7,
        out_specs=pl.BlockSpec(memory_space=pltpu.VMEM),
        scratch_shapes=[
            pltpu.VMEM((3 * L, 16, 128), F32),
            pltpu.VMEM((3 * L, 8, 128), F32),
            pltpu.VMEM((L, 64, 128), F32),
            pltpu.VMEM((L, 3, 128, 128), F32),
            pltpu.VMEM((L, 4, 64, 64), F32),
            pltpu.VMEM((L, 64, 64), F32),
            pltpu.VMEM((1, 64, 64), F32),
            pltpu.VMEM((1, 16, 64, 64), F32),
            pltpu.VMEM((CS * XS * ZS, 8, 128), F32),
            pltpu.VMEM((YS, 8, 128), F32),
            pltpu.VMEM((16, 64, 64), BF16),
            pltpu.VMEM((16, 64, 64), BF16),
            pltpu.VMEM((L, 192, 128), BF16),
            pltpu.VMEM((L, 256, 256), BF16),
            pltpu.VMEM((L, 256, 128), BF16),
            pltpu.VMEM((L, 64, 256), BF16),
            pltpu.SemaphoreType.DMA((3 * CHUNKS + 4,)),
            pltpu.SemaphoreType.DMA((4,)),
            pltpu.SemaphoreType.DMA((4,)),
            pltpu.SemaphoreType.DMA((XS * ZS,)),
            pltpu.SemaphoreType.DMA((XS * ZS,)),
            pltpu.SemaphoreType.DMA((YS,)),
            pltpu.SemaphoreType.DMA((YS,)),
            pltpu.SemaphoreType.DMA((XS,)),
            pltpu.SemaphoreType.DMA((XS,)),
        ],
        compiler_params=pltpu.CompilerParams(
            collective_id=0, has_side_effects=True, vmem_limit_bytes=56 * 1024 * 1024
        ),
    )(
        near_index.T,
        coupling_index.T,
        branch_index,
        vectors,
        leaf_basis,
        near_blocks,
        coupling_blocks,
        leaf_transfer,
        cluster_transfer,
        branch_blocks,
    )
    result = pltpu.with_memory_space_constraint(result, pltpu.VMEM)
    return pl.pallas_call(
        store,
        name="store",
        out_shape=jax.ShapeDtypeStruct((L, 16, 128), F32),
        in_specs=[pl.BlockSpec(memory_space=pltpu.VMEM)],
        out_specs=anywhere,
        scratch_shapes=[pltpu.SemaphoreType.DMA],
    )(result)


def solution(mesh):
    rows = ("branch", "sub")
    in_specs = (
        P(rows, None, None),
        P(rows, None, None),
        P(rows, None),
        P(rows, None, None, None),
        P(rows, None),
        P(rows, None, None, None),
        P(rows, None, None),
        P(rows, None, None),
        P("branch", None),
        P("branch", None, None, None),
    )
    return jax.shard_map(
        per_device, mesh=mesh, in_specs=in_specs, out_specs=P(rows, None, None), check_vma=False
    )
```

```python
import jax
import jax.numpy as jnp
from jax import lax
from jax.experimental import pallas as pl
from jax.experimental.pallas import tpu as pltpu
from jax.sharding import PartitionSpec as P

MESH = pl.DeviceIdType.MESH
NT = (((1,), (1,)), ((), ()))
NN = (((1,), (0,)), ((), ()))
XS, ZS, CS, YS = 4, 8, 2, 4
L = 36
CHUNKS = 3
PART = L // CHUNKS
GROUP = 12
F32, BF16 = jnp.float32, jnp.bfloat16


def split(x):
    hi = x.astype(BF16)
    lo = (x - hi.astype(F32)).astype(BF16)
    return hi, lo


def stack(x):
    return jnp.concatenate(split(x), axis=0)


def mm(a, b, dims):
    return lax.dot_general(a, b, dims, preferred_element_type=F32)


def dot3(a, b, dims):
    return dot3_split(a, *split(b), dims)


def dot3_split(a, bh, bl, dims):
    ah, al = split(a)
    rows = a.shape[0]
    both = mm(jnp.concatenate([ah, al], axis=0), bh, dims)
    return both[:rows] + (both[rows:] + mm(ah, bl, dims))


def pack(c):
    return jnp.concatenate([c[:8], c[8:]], axis=1)


def unpack(p):
    return jnp.concatenate([p[:, :64], p[:, 64:]], axis=0)


def pair(p, q):
    low = lax.broadcasted_iota(jnp.int32, p.shape, 1) < 64
    top = jnp.where(low, p, pltpu.roll(q, 64, 1))
    bottom = jnp.where(low, pltpu.roll(p, 64, 1), q)
    return jnp.concatenate([top, bottom], axis=0)


def fold(s):
    half = s.shape[1] // 2
    both = s[:16] + s[16:]
    return both[:, :half] + both[:, half:]


def wide_split(x):
    hi = x.astype(BF16).astype(F32)
    return jnp.concatenate([hi, x - hi], axis=1).astype(BF16)


def groups(body, size=GROUP):
    def step(g, carry):
        body([g * size + i for i in range(size)])
        return carry

    lax.fori_loop(0, L // size, step, 0)


def kernel(
    near_index,
    coup_index,
    branch_index,
    vec_hbm,
    basis_hbm,
    near_hbm,
    coup_hbm,
    lt_hbm,
    ct_hbm,
    bb_hbm,
    out,
    wide,
    cw,
    basis,
    near,
    coup,
    lt,
    ct,
    bb,
    nodes,
    fars,
    bbh,
    bbl,
    down,
    near12,
    coup4,
    basis2,
    local_sem,
    halo_send,
    halo_recv,
    node_send,
    node_recv,
    far_send,
    far_recv,
    pair_send,
    pair_recv,
):
    b = lax.axis_index("branch")
    y = lax.axis_index("sub")
    core = lax.rem(b, CS)
    z = lax.rem(lax.div(b, CS), ZS)
    x = lax.div(b, CS * ZS)
    flat = b * YS + y
    total = XS * ZS * CS * YS
    right = lax.rem(flat + 1, total)
    left = lax.rem(flat + total - 1, total)
    right = (lax.div(right, YS), lax.rem(right, YS))
    left = (lax.div(left, YS), lax.rem(left, YS))
    mine = x * ZS + z
    slot = core * XS * ZS + mine
    sibling = (b + 1 - 2 * core, y)

    def plane_peer(j):
        px = lax.rem(x + lax.div(j, ZS), XS)
        pz = lax.rem(z + lax.rem(j, ZS), ZS)
        return ((px * ZS + pz) * CS + core, y)

    def far_first(n):
        q = lax.div(n, XS)
        sign = 1 - 2 * lax.rem(q, 2)
        dz = lax.rem(ZS // 2 + sign * lax.div(q + 1, 2) + ZS, ZS)
        return (XS - 1 - lax.rem(n, XS)) * ZS + dz

    def row_peer(j):
        return (b, lax.rem(y + j, YS))

    def local(src, dst, n):
        return pltpu.make_async_copy(src, dst, local_sem.at[n])

    barrier = pltpu.get_barrier_semaphore()

    def greet(peer):
        pl.semaphore_signal(barrier, inc=1, device_id=peer, device_id_type=MESH)


    def greet_plane(n, carry):
        greet(plane_peer(far_first(n)))
        return carry

    def greet_row(j, carry):
        greet(row_peer(j))
        return carry

    lax.fori_loop(0, XS * ZS - 1, greet_plane, 0)
    greet(right)
    greet(left)
    greet(sibling)
    lax.fori_loop(1, YS, greet_row, 0)

    first = []
    for i in range(CHUNKS):
        part = pl.ds(i * PART, PART)
        first.append(
            [
                local(vec_hbm.at[part], wide.at[pl.ds(L + i * PART, PART)], 3 * i),
                local(basis_hbm.at[part], basis.at[part], 3 * i + 1),
                local(lt_hbm.at[part], lt.at[part], 3 * i + 2),
            ]
        )
    for loads in first:
        for load in loads:
            load.start()
    n = 3 * CHUNKS
    ct_load = local(ct_hbm, ct, n)
    bb_load = local(bb_hbm, bb, n + 1)
    near_load = local(near_hbm, near, n + 2)
    coup_load = local(coup_hbm, coup, n + 3)
    for load in (ct_load, bb_load, near_load, coup_load):
        load.start()

    acc = jnp.zeros((32, 128), F32)
    for i in range(CHUNKS):
        for load in first[i]:
            load.wait()
        ls = range(i * PART, (i + 1) * PART)
        cs = [dot3(wide[L + l], basis[l], NT) for l in ls]
        for l, c in zip(ls, cs):
            cw[L + l] = pack(c)
        for l, c in zip(ls, cs):
            acc = acc + mm(stack(c), stack(lt[l]), NT)
    cluster = (acc[:16, :64] + acc[16:, :64]) + (acc[:16, 64:] + acc[16:, 64:])
    ct_load.wait()
    nodes[slot] = pack(dot3(cluster, ct[0], NT))

    pl.semaphore_wait(barrier, 3 + (XS * ZS - 1) + (YS - 1))

    def remote(src, dst, send, recv, peer):
        return pltpu.make_async_remote_copy(
            src_ref=src, dst_ref=dst, send_sem=send, recv_sem=recv, device_id=peer, device_id_type=MESH
        )

    def node_copy(j):
        return remote(
            nodes.at[slot], nodes.at[slot], node_send.at[j], node_recv.at[j], plane_peer(j)
        )

    def far_copy(j):
        return remote(fars.at[y], fars.at[y], far_send.at[j], far_recv.at[j], row_peer(j))

    def pair_copy(j):
        rows = pl.ds((core * XS + lax.rem(x + j, XS)) * ZS, ZS)
        return remote(nodes.at[rows], nodes.at[rows], pair_send.at[j], pair_recv.at[j], sibling)

    def each(lo, hi, body):
        def step(j, carry):
            body(j)
            return carry

        lax.fori_loop(lo, hi, step, 0)

    vec_halo = [
        remote(vec_hbm, wide.at[pl.ds(0, L)], halo_send.at[0], halo_recv.at[0], right),
        remote(vec_hbm, wide.at[pl.ds(2 * L, L)], halo_send.at[1], halo_recv.at[1], left),
    ]
    coeff_halo = [
        remote(cw.at[pl.ds(L, L)], cw.at[pl.ds(0, L)], halo_send.at[2], halo_recv.at[2], right),
        remote(cw.at[pl.ds(L, L)], cw.at[pl.ds(2 * L, L)], halo_send.at[3], halo_recv.at[3], left),
    ]
    early = z < ZS // 2

    def start_halos():
        for copy in coeff_halo + vec_halo:
            copy.start()

    pl.when(early)(start_halos)
    each(0, XS * ZS - 1, lambda n: node_copy(far_first(n)).start())
    pl.when(jnp.logical_not(early))(start_halos)

    bb_load.wait()
    for k in range(16):
        bbh[k], bbl[k] = split(bb[0, k])

    def down_step(ls):
        for l in ls:
            step = dot3(dot3(ct[0], lt[l], NN), basis[l], NN)
            hi, lo = split(step)
            down[l, 0:64] = hi
            down[l, 64:128] = hi
            down[l, 128:192] = lo

    groups(down_step)

    near_load.wait()

    def near_own(ls):
        for l in ls:
            out[l] = dot3(wide[L + l], near[l, 0], NT)
        for l in ls:
            for k in (1, 2):
                near12[l, (k - 1) * 128 : k * 128] = wide_split(near[l, k].T)

    groups(near_own)

    coup_load.wait()

    def coup_own(ls):
        for l in ls:
            for k in range(4):
                coup4[l, k * 64 : (k + 1) * 64] = wide_split(coup[l, k].T)
            basis2[l] = wide_split(basis[l])

    groups(coup_own)

    anchor = flat * L - L

    def place(index):
        return jnp.clip(index - anchor, 0, 3 * L - 1)

    for copy in coeff_halo:
        copy.wait_recv()

    def far_step(ls):
        totals = []
        for l in ls:
            p = [cw[place(coup_index[k, l])] for k in range(4)]
            rows = stack(jnp.concatenate([pair(p[0], p[1]), pair(p[2], p[3])], axis=1))
            totals.append(fold(mm(rows, coup4[l], NN)))
        for l, acc in zip(ls, totals):
            out[l] = out[l] + fold(mm(stack(acc), basis2[l], NN))

    groups(far_step, 36)

    for j in (0, 1, 3, 2):
        each(j * ZS + (j == 0), (j + 1) * ZS, lambda n: node_copy(n).wait_recv())
        pair_copy((XS - j) % XS).start()
    each(0, XS, lambda j: pair_copy(j).wait_recv())

    far = jnp.zeros((16, 64), F32)
    for k in range(16):
        i = branch_index[0, k]
        node = nodes[lax.rem(i, CS) * (XS * ZS) + lax.div(i, CS)]
        far = far + dot3_split(unpack(node), bbh[k], bbl[k], NT)
    fars[y] = pack(far)
    each(1, YS, lambda j: far_copy(j).start())

    each(1, XS * ZS, lambda j: node_copy(j).wait_send())
    each(0, XS, lambda j: pair_copy(j).wait_send())
    for copy in coeff_halo:
        copy.wait_send()
    for copy in vec_halo:
        copy.wait_recv()

    def near_step(ls):
        for l in ls:
            h1, l1 = split(wide[place(near_index[1, l])])
            h2, l2 = split(wide[place(near_index[2, l])])
            rows = jnp.concatenate(
                [jnp.concatenate([h1, h2], axis=1), jnp.concatenate([l1, l2], axis=1)], axis=0
            )
            out[l] = out[l] + fold(mm(rows, near12[l], NN))

    groups(near_step, 36)

    each(1, YS, lambda j: far_copy(j).wait_recv())
    far = unpack((fars[0] + fars[1]) + (fars[2] + fars[3]))
    fh, fl = split(far)
    flh = jnp.concatenate([fh, fl, fh], axis=1)
    for l in range(L):
        out[l] = out[l] + mm(flh, down[l], NN)

    for copy in vec_halo:
        copy.wait_send()
    each(1, YS, lambda j: far_copy(j).wait_send())


def store(source, target, sem):
    copy = pltpu.make_async_copy(source, target, sem)
    copy.start()
    copy.wait()


def per_device(
    vectors,
    leaf_basis,
    near_index,
    near_blocks,
    coupling_index,
    coupling_blocks,
    leaf_transfer,
    cluster_transfer,
    branch_index,
    branch_blocks,
):
    smem = pl.BlockSpec(memory_space=pltpu.SMEM)
    anywhere = pl.BlockSpec(memory_space=pl.ANY)
    result = pl.pallas_call(
        kernel,
        name="h2_product",
        out_shape=pltpu.VMEM((L, 16, 128), F32),
        in_specs=[smem] * 3 + [anywhere] * 7,
        out_specs=pl.BlockSpec(memory_space=pltpu.VMEM),
        scratch_shapes=[
            pltpu.VMEM((3 * L, 16, 128), F32),
            pltpu.VMEM((3 * L, 8, 128), F32),
            pltpu.VMEM((L, 64, 128), F32),
            pltpu.VMEM((L, 3, 128, 128), F32),
            pltpu.VMEM((L, 4, 64, 64), F32),
            pltpu.VMEM((L, 64, 64), F32),
            pltpu.VMEM((1, 64, 64), F32),
            pltpu.VMEM((1, 16, 64, 64), F32),
            pltpu.VMEM((CS * XS * ZS, 8, 128), F32),
            pltpu.VMEM((YS, 8, 128), F32),
            pltpu.VMEM((16, 64, 64), BF16),
            pltpu.VMEM((16, 64, 64), BF16),
            pltpu.VMEM((L, 192, 128), BF16),
            pltpu.VMEM((L, 256, 256), BF16),
            pltpu.VMEM((L, 256, 128), BF16),
            pltpu.VMEM((L, 64, 256), BF16),
            pltpu.SemaphoreType.DMA((3 * CHUNKS + 4,)),
            pltpu.SemaphoreType.DMA((4,)),
            pltpu.SemaphoreType.DMA((4,)),
            pltpu.SemaphoreType.DMA((XS * ZS,)),
            pltpu.SemaphoreType.DMA((XS * ZS,)),
            pltpu.SemaphoreType.DMA((YS,)),
            pltpu.SemaphoreType.DMA((YS,)),
            pltpu.SemaphoreType.DMA((XS,)),
            pltpu.SemaphoreType.DMA((XS,)),
        ],
        compiler_params=pltpu.CompilerParams(
            collective_id=0, has_side_effects=True, vmem_limit_bytes=56 * 1024 * 1024
        ),
    )(
        near_index.T,
        coupling_index.T,
        branch_index,
        vectors,
        leaf_basis,
        near_blocks,
        coupling_blocks,
        leaf_transfer,
        cluster_transfer,
        branch_blocks,
    )
    result = pltpu.with_memory_space_constraint(result, pltpu.VMEM)
    return pl.pallas_call(
        store,
        name="store",
        out_shape=jax.ShapeDtypeStruct((L, 16, 128), F32),
        in_specs=[pl.BlockSpec(memory_space=pltpu.VMEM)],
        out_specs=anywhere,
        scratch_shapes=[pltpu.SemaphoreType.DMA],
    )(result)


def solution(mesh):
    rows = ("branch", "sub")
    in_specs = (
        P(rows, None, None),
        P(rows, None, None),
        P(rows, None),
        P(rows, None, None, None),
        P(rows, None),
        P(rows, None, None, None),
        P(rows, None, None),
        P(rows, None, None),
        P("branch", None),
        P("branch", None, None, None),
    )
    return jax.shard_map(
        per_device, mesh=mesh, in_specs=in_specs, out_specs=P(rows, None, None), check_vma=False
    )
```
